32 devices in a mesh: seq: 16 (over z, y, x), batch: 2 (over core).
Axes of the slice: x: 2, y: 2, z: 4, core: 2. Of those that a mesh axis runs over, the one named last changes fastest.
Arguments:
- tokens: bfloat16 [2, 16384, 768], P('batch', 'seq'), may hold values from -6 to 6
- global_states: bfloat16 [2, 128, 768], P('batch'), may hold values from -6 to 6
- doc_starts: int32 [2, 8], P('batch'), may hold values from 0 to 16383, as said below
- doc_lengths: int32 [2, 8], P('batch'), may hold values from 1 to 8192, as said below
- first_gain: float32 [768], replicated, may hold values from 0.5 to 1.5
- first_bias: float32 [768], replicated, may hold values from -3 to 3
- query_weight: bfloat16 [768, 768], replicated, may hold values from -0.4375 to 0.4375
- key_weight: bfloat16 [768, 768], replicated, may hold values from -0.21875 to 0.21875
- value_weight: bfloat16 [768, 768], replicated, may hold values from -0.21875 to 0.21875
- output_weight: bfloat16 [768, 768], replicated, may hold values from -3.5 to 3.5
- second_gain: float32 [768], replicated, may hold values from 0.5 to 1.5
- second_bias: float32 [768], replicated, may hold values from -3 to 3
- hidden_weight: bfloat16 [768, 3072], replicated, may hold values from -0.21875 to 0.21875
- return_weight: bfloat16 [3072, 768], replicated, may hold values from -0.21875 to 0.21875
- output_cotangent: bfloat16 [2, 16384, 768], P('batch', 'seq'), may hold values from -6 to 6
- global_cotangent: bfloat16 [2, 128, 768], P('batch'), may hold values from -6 to 6
Outputs:
- block_out: bfloat16 [2, 16384, 768], P('batch', 'seq')
- global_out: bfloat16 [2, 128, 768], P('batch')
- tokens_grad: float32 [2, 16384, 768], P('batch', 'seq')
- global_grad: float32 [2, 128, 768], P('batch')
- first_gain_grad: float32 [768], P(('seq', 'batch'))
- first_bias_grad: float32 [768], P(('seq', 'batch'))
- query_grad: float32 [768, 768], P(('seq', 'batch'))
- key_grad: float32 [768, 768], P(('seq', 'batch'))
- value_grad: float32 [768, 768], P(('seq', 'batch'))
- output_grad: float32 [768, 768], P(('seq', 'batch'))
- second_gain_grad: float32 [768], P(('seq', 'batch'))
- second_bias_grad: float32 [768], P(('seq', 'batch'))
- hidden_grad: float32 [768, 3072], P(('seq', 'batch'))
- return_grad: float32 [3072, 768], P(('seq', 'batch'))
The draws below stay inside these ranges and needn't reach their ends.
Inputs may be any that keep to these rules, and one draw needn't show every extreme that they name: `doc_starts`: documents of a group lie in increasing order and are disjoint; the first starts at token 0 and the last ends at token 16383; each but the last two is followed by at most 64 padding tokens. `doc_lengths`: each group holds one document of exactly 8192 tokens; the others are short.
All inputs are finite; a program needn't handle non-finite values.
Results may differ from the reference program's by a relative error of at most 0.012.
The reference program's roundings to bfloat16 on the way count: a program that leaves them out, or rounds other values in their place, can miss the bound.
Values may be sent and summed in bfloat16 or wider, within the bound.
No kernel may reach another device: no remote copies, remote signals or barrier semaphores. Data moves between devices by JAX's collectives and lax.ppermute only.
A program may use at most 320 MiB of HBM per device.

```python
import jax
import jax.numpy as jnp
from jax import lax

D = 768
HEADS = 12
HEAD_DIM = 64
FF = 3072
BLOCK = 512
NG = 128
PAD_MOST = 64
HALF = 256
TOKENS = 16384
GROUPS = 2
MAX_DOC = 8192
NDOCS = 8


def document_layout(key):
    spread = max(1, (TOKENS - MAX_DOC - NDOCS * PAD_MOST) // (NDOCS - 1))
    lowest = max(1, 3 * spread // 4)

    def one_group(group_key):
        lengths = jax.random.randint(jax.random.fold_in(group_key, 11), (NDOCS,), lowest, spread + 1)
        longest = jax.random.randint(jax.random.fold_in(group_key, 12), (), 0, NDOCS)
        lengths = jnp.where(jnp.arange(NDOCS) == longest, MAX_DOC, jnp.minimum(lengths, MAX_DOC))
        gaps = jax.random.randint(jax.random.fold_in(group_key, 13), (NDOCS,), 0, PAD_MOST + 1)
        ends = jnp.cumsum(lengths + gaps) - gaps
        slack = TOKENS - ends[NDOCS - 1]
        starts = ends - lengths + jnp.where(jnp.arange(NDOCS) == NDOCS - 1, slack, 0)
        return (starts.astype(jnp.int32), lengths.astype(jnp.int32))
    group_keys = jnp.stack([jax.random.fold_in(key, 100 + group_index) for group_index in range(GROUPS)])
    return jax.vmap(one_group)(group_keys)


def draw_doc_starts(key, part):
    return document_layout(key)[0]


def draw_doc_lengths(key, part):
    return document_layout(key)[1]


def levels(rng, shape, cuts, least, top_value):
    loudness = 1.0
    for dim, shards_of in cuts:
        heights = jax.random.uniform(jax.random.fold_in(jax.random.fold_in(rng, 6), dim), (shards_of,), jnp.float32, least / len(cuts), top_value / len(cuts))
        loudness = loudness * jnp.repeat(jnp.exp(heights), shape[dim] // shards_of).reshape((-1,) + (1,) * (len(shape) - 1 - dim))
    return loudness


def bell_draw(rng, shape, width, bound, cuts=(), kind=jnp.bfloat16):
    values = jax.random.normal(rng, shape, jnp.float32) * width
    if len(cuts) > 0:
        values = levels(rng, shape, cuts, -0.22, 0.18) * values
    return jnp.clip(values, min=-bound, max=bound).astype(kind)


def setup_inputs(seed: int = 0) -> dict:
    key_of = jax.random.split(jax.random.key(seed), 17)
    tokens = bell_draw(key_of[0], (GROUPS, TOKENS, D), 1.0, 6.0, ((0, 2), (1, 16)))
    global_states = bell_draw(key_of[1], (GROUPS, NG, D), 1.0, 6.0, ((0, 2),))
    doc_starts = draw_doc_starts(jax.random.fold_in(key_of[16], 71), 0)
    doc_lengths = draw_doc_lengths(jax.random.fold_in(key_of[16], 71), 0)
    first_gain = jnp.clip(1.0 + 0.1 * jax.random.normal(key_of[4], (D,), jnp.float32), 0.5, 1.5)
    first_bias = bell_draw(key_of[5], (D,), 0.5, 3.0, (), jnp.float32)
    query_weight = bell_draw(key_of[6], (D, D), (D // 4) ** -0.5, 0.4375)
    key_weight = bell_draw(key_of[7], (D, D), D ** -0.5, 0.21875)
    value_weight = bell_draw(key_of[8], (D, D), D ** -0.5, 0.21875)
    output_weight = bell_draw(key_of[9], (D, D), (D // 256) ** -0.5, 3.5)
    second_gain = jnp.clip(1.0 + 0.1 * jax.random.normal(key_of[10], (D,), jnp.float32), 0.5, 1.5)
    second_bias = bell_draw(key_of[11], (D,), 0.5, 3.0, (), jnp.float32)
    hidden_weight = bell_draw(key_of[12], (D, FF), D ** -0.5, 0.21875)
    return_weight = bell_draw(key_of[13], (FF, D), (FF // 4) ** -0.5, 0.21875)
    output_cotangent = bell_draw(key_of[14], (GROUPS, TOKENS, D), 1.0, 6.0, ((0, 2), (1, 16)))
    global_cotangent = bell_draw(key_of[15], (GROUPS, NG, D), 1.0, 6.0, ((0, 2),))
    return dict(tokens=tokens, global_states=global_states, doc_starts=doc_starts, doc_lengths=doc_lengths, first_gain=first_gain, first_bias=first_bias, query_weight=query_weight, key_weight=key_weight, value_weight=value_weight, output_weight=output_weight, second_gain=second_gain, second_bias=second_bias, hidden_weight=hidden_weight, return_weight=return_weight, output_cotangent=output_cotangent, global_cotangent=global_cotangent)


epsilon = 1e-05
scale_factor = 0.125
masked_value = -1e+30
highest = lax.Precision.HIGHEST

@jax.custom_vjp
def low(v):
    return lax.optimization_barrier(v.astype(jnp.bfloat16)).astype(jnp.float32)

@jax.custom_vjp
def low_back(v):
    return v

def low_keep(v):
    return (low(v), None)

def low_pass(kept, grad):
    return (grad,)

def back_keep(v):
    return (v, None)

def back_low(kept, grad):
    return (low(grad),)
low.defvjp(low_keep, low_pass)
low_back.defvjp(back_keep, back_low)

def layer_norm(value, gain, bias):
    center = value - lax.optimization_barrier(jnp.mean(value, axis=-1, keepdims=True))
    spread = lax.optimization_barrier(jnp.mean(center * center, axis=-1, keepdims=True))
    return center * lax.rsqrt(spread + epsilon) * gain + bias

def matmul(left, right):
    return jnp.dot(left, right, precision=highest)

def project(normed, weight):
    return low(low_back(matmul(normed, weight)))

def document_ids(positions, starts, lengths):
    inside = (positions[:, None] >= starts[None, :]) & (positions[:, None] < (starts + lengths)[None, :])
    numbers = jnp.arange(1, starts.shape[0] + 1, dtype=jnp.int32)
    return lax.optimization_barrier(jnp.sum(jnp.where(inside, numbers[None, :], 0), axis=1)).astype(jnp.int32)

def group_forward(inputs, glob, ident_pad, params):
    first_gain, first_bias, query_weight, key_weight, value_weight, output_weight, second_gain, second_bias, hidden_weight, return_weight = params
    normed = low(layer_norm(inputs, first_gain, first_bias))
    normed_glob = low(layer_norm(glob, first_gain, first_bias))
    queries = project(normed, query_weight)
    key_rows = project(normed, key_weight)
    value_rows = project(normed, value_weight)
    query_glob = project(normed_glob, query_weight)
    key_glob = project(normed_glob, key_weight)
    value_glob = project(normed_glob, value_weight)
    key_glob_heads = key_glob.reshape(NG, HEADS, HEAD_DIM)
    value_glob_heads = value_glob.reshape(NG, HEADS, HEAD_DIM)
    padding = jnp.zeros((HALF, D), jnp.float32)

    def blocks(value):
        return jnp.concatenate([padding, value, padding]).reshape(-1, BLOCK, D)

    def attend(pieces):
        query_block, key_block, value_block, ident_block = pieces
        query_heads = query_block.reshape(BLOCK, HEADS, HEAD_DIM)
        near_scores = jnp.einsum('qhd,khd->hqk', query_heads, key_block.reshape(BLOCK, HEADS, HEAD_DIM), precision=highest) * scale_factor
        far_scores = jnp.einsum('qhd,khd->hqk', query_heads, key_glob_heads, precision=highest) * scale_factor
        scores = low_back(jnp.concatenate([near_scores, far_scores], axis=-1))
        allowed = (ident_block[:, None] == ident_block[None, :]) & (ident_block[None, :] > 0)
        allowed = jnp.concatenate([allowed, jnp.ones((BLOCK, NG), jnp.bool_)], axis=-1)
        scores = jnp.where(allowed[None], scores, masked_value)
        probs = low(jax.nn.softmax(scores, axis=-1))
        stacked = jnp.concatenate([value_block.reshape(BLOCK, HEADS, HEAD_DIM), value_glob_heads], axis=0)
        return jnp.einsum('hqk,khd->qhd', probs, stacked, precision=highest).reshape(BLOCK, D)
    local_out = lax.map(jax.checkpoint(attend), (blocks(queries), blocks(key_rows), blocks(value_rows), ident_pad.reshape(-1, BLOCK)))
    local_out = local_out.reshape(-1, D)[HALF:HALF + TOKENS]
    ident = ident_pad[HALF:HALF + TOKENS]
    glob_heads = query_glob.reshape(NG, HEADS, HEAD_DIM)
    own_scores = jnp.einsum('ghd,khd->hgk', glob_heads, key_rows.reshape(TOKENS, HEADS, HEAD_DIM), precision=highest) * scale_factor
    self_scores = jnp.einsum('ghd,khd->hgk', glob_heads, key_glob_heads, precision=highest) * scale_factor
    scores = low_back(jnp.concatenate([own_scores, self_scores], axis=-1))
    allowed = jnp.concatenate([ident > 0, jnp.ones((NG,), jnp.bool_)])
    scores = jnp.where(allowed[None, None, :], scores, masked_value)
    probs = low(jax.nn.softmax(scores, axis=-1))
    stacked = jnp.concatenate([value_rows.reshape(TOKENS, HEADS, HEAD_DIM), value_glob_heads], axis=0)
    glob_out = jnp.einsum('hgk,khd->ghd', probs, stacked, precision=highest).reshape(NG, D)
    attended = low(low_back(jnp.concatenate([local_out, glob_out])))
    resid = jnp.concatenate([inputs, glob]) + low_back(matmul(attended, output_weight))
    normed_two = low(layer_norm(resid, second_gain, second_bias))
    pre_act = low_back(matmul(normed_two, hidden_weight))
    activ = low(jax.nn.gelu(pre_act, approximate=False))
    result = resid + low_back(matmul(activ, return_weight))
    return (result[:TOKENS], result[TOKENS:])

def reference(tokens, global_states, doc_starts, doc_lengths, first_gain, first_bias, query_weight, key_weight, value_weight, output_weight, second_gain, second_bias, hidden_weight, return_weight, output_cotangent, global_cotangent):
    params = (first_gain.astype(jnp.float32), first_bias.astype(jnp.float32), query_weight.astype(jnp.float32), key_weight.astype(jnp.float32), value_weight.astype(jnp.float32), output_weight.astype(jnp.float32), second_gain.astype(jnp.float32), second_bias.astype(jnp.float32), hidden_weight.astype(jnp.float32), return_weight.astype(jnp.float32))
    positions = jnp.arange(TOKENS + BLOCK, dtype=jnp.int32) - HALF
    idents = [document_ids(positions, doc_starts[group_index], doc_lengths[group_index]) for group_index in range(GROUPS)]

    def forward(inputs, globs, weights):
        token_outs = []
        glob_outs = []
        for group_index in range(GROUPS):
            token_part, glob_part = group_forward(inputs[group_index], globs[group_index], idents[group_index], weights)
            token_outs.append(token_part)
            glob_outs.append(glob_part)
        return (jnp.stack(token_outs), jnp.stack(glob_outs))
    outputs, pullback = jax.vjp(forward, tokens.astype(jnp.float32), global_states.astype(jnp.float32), params)
    tokens_grad, global_grad, weight_grads = pullback((output_cotangent.astype(jnp.float32), global_cotangent.astype(jnp.float32)))
    return (outputs[0].astype(jnp.bfloat16), outputs[1].astype(jnp.bfloat16), tokens_grad, global_grad, weight_grads[0], weight_grads[1], weight_grads[2], weight_grads[3], weight_grads[4], weight_grads[5], weight_grads[6], weight_grads[7], weight_grads[8], weight_grads[9])
```

```python
import jax
import jax.numpy as jnp
from jax import lax
from jax.experimental import pallas as pl
from jax.experimental.pallas import tpu as pltpu
from jax.sharding import PartitionSpec as P

HEADS = 12
HEAD_DIM = 64
PAIRS = HEADS // 2
LANES = 2 * HEAD_DIM
BLOCK = 512
NG = 128
HALF = 256

EPSILON = 1e-05
SCALE = 0.125
MASKED = -1e30
INV_SQRT2 = 0.7071067811865476
INV_SQRT2PI = 0.3989422804014327
bf16, f32 = jnp.bfloat16, jnp.float32


def nn(left, right):
    return jnp.dot(left, right, preferred_element_type=f32)


def nt(left, right):
    return lax.dot_general(left, right, (((1,), (1,)), ((), ())), preferred_element_type=f32)


def tn(left, right):
    return lax.dot_general(left, right, (((0,), (0,)), ((), ())), preferred_element_type=f32)


def head_lanes(value, head):
    lane = lax.broadcasted_iota(jnp.int32, value.shape, 1)
    return jnp.where((lane >= HEAD_DIM) == (head == 1), value, jnp.zeros_like(value))


def same_doc(key_col, query_row):
    return jnp.where((key_col == query_row) & (key_col > 0), 0.0, MASKED)


def attend(query, keys, values_t, biases):
    outs = []
    for head in (0, 1):
        one = head_lanes(query, head)
        scores = [nt(key, one) for key in keys]
        scores = [s if b is None else s + b[...] for s, b in zip(scores, biases)]
        peak = scores[0].max(0, keepdims=True)
        for s in scores[1:]:
            peak = jnp.maximum(peak, s.max(0, keepdims=True))
        probs = [jnp.exp(s - peak) for s in scores]
        total = sum(p.sum(0, keepdims=True) for p in probs)
        rows = slice(HEAD_DIM * head, HEAD_DIM * (head + 1))
        out = sum(nn(v[rows, :], p.astype(bf16)) for v, p in zip(values_t, probs))
        outs.append((out, peak, total))
    return outs


def put_local(outs, out_ref, lse_ref, rows):
    joined = jnp.concatenate([out * (1.0 / total) for out, _, total in outs], axis=0)
    out_ref[rows, :] = joined.T.astype(bf16)
    for head, (_, peak, total) in enumerate(outs):
        lse_ref[0, head : head + 1, rows] = peak + jnp.log(total)


def forward_mid_kernel(
    q_ref, k_ref, v_ref, qg_ref, kg_ref, vg_ref, idc_ref, idr_ref, kb_ref,
    out_ref, lse_ref, outg_ref, stat_ref, bias, gbias,
):
    rows = q_ref.shape[0]
    mid = slice(HALF, rows - HALF)

    @pl.when(pl.program_id(0) == 0)
    def _():
        bias[...] = same_doc(idc_ref[mid, :], idr_ref[:, mid])
        gbias[...] = jnp.broadcast_to(kb_ref[...], gbias.shape)

    kg = kg_ref[...]
    vt, vgt = v_ref[...].T, vg_ref[...].T
    outs = attend(q_ref[mid, :] * bf16(SCALE), [k_ref[mid, :], kg], [vt[:, mid], vgt], [bias, None])
    put_local(outs, out_ref, lse_ref, slice(0, rows - BLOCK))
    outs = attend(
        qg_ref[...] * bf16(SCALE), [k_ref[...], kg], [vt, vgt], [gbias.at[:rows], gbias.at[rows:]]
    )
    outg_ref[...] = jnp.concatenate([out for out, _, _ in outs], axis=0).T
    for head, (_, peak, total) in enumerate(outs):
        stat_ref[0, head : head + 1, :] = peak
        stat_ref[0, 2 + head : 3 + head, :] = total


def edge_slices(rows):
    sides = (slice(0, HALF), slice(rows - HALF, rows))
    return zip(sides, (slice(0, HALF), slice(HALF, BLOCK)))


def edge_biases(idc_ref, idr_ref, idh_ref, own, halo):
    for side, half in edge_slices(idc_ref.shape[0]):
        own[half, :] = same_doc(idc_ref[side, :], idr_ref[:, side])
        halo[half, :] = same_doc(idh_ref[half, :], idr_ref[:, side])


def forward_edge_kernel(
    q_ref, k_ref, v_ref, kh_ref, vh_ref, kg_ref, vg_ref, idc_ref, idr_ref, idh_ref,
    out_ref, lse_ref, own, halo,
):
    @pl.when(pl.program_id(0) == 0)
    def _():
        edge_biases(idc_ref, idr_ref, idh_ref, own, halo)

    kg, vgt = kg_ref[...], vg_ref[...].T
    for side, half in edge_slices(q_ref.shape[0]):
        outs = attend(
            q_ref[side, :] * bf16(SCALE),
            [k_ref[side, :], kh_ref[half, :], kg],
            [v_ref[side, :].T, vh_ref[half, :].T, vgt],
            [own.at[half], halo.at[half], None],
        )
        put_local(outs, out_ref, lse_ref, half)


def attend_back(query, grad, lse, delta, keys, keys_t, values, biases):
    queries, grads, all_probs, all_dscores, grad_queries = [], [], [], [], []
    for head in (0, 1):
        one, grad_one = head_lanes(query, head), head_lanes(grad, head)
        probs = []
        for key, bias in zip(keys, biases):
            score = nt(key, one) - lse[head]
            if bias is not None:
                score = score + bias[...]
            probs.append(jnp.exp(score))
        dscores = [
            (p * (nt(v, grad_one) - delta[head])).astype(bf16) for p, v in zip(probs, values)
        ]
        all_probs.append([p.astype(bf16) for p in probs])
        all_dscores.append(dscores)
        queries.append(one)
        grads.append(grad_one)
        rows = slice(HEAD_DIM * head, HEAD_DIM * (head + 1))
        grad_queries.append(sum(nn(k[rows, :], d) for k, d in zip(keys_t, dscores)))
    grad_query = jnp.concatenate(grad_queries, axis=0) * SCALE
    parts = range(len(keys))
    grad_keys = [nn(all_dscores[0][i], queries[0]) + nn(all_dscores[1][i], queries[1]) for i in parts]
    grad_values = [nn(all_probs[0][i], grads[0]) + nn(all_probs[1][i], grads[1]) for i in parts]
    return grad_query, grad_keys, grad_values


def backward_kernel(
    q_ref, k_ref, v_ref, qg_ref, kg_ref, vg_ref, kh_ref, vh_ref, do_ref, o_ref, dog_ref,
    lse_ref, stat_ref, idc_ref, idr_ref, idh_ref, kb_ref,
    dq_ref, dk_ref, dv_ref, dkh_ref, dvh_ref,
    bmid, own, halo, gbias, dk_sum, dv_sum,
):
    rows = q_ref.shape[0]
    mid = slice(HALF, rows - HALF)
    glob = slice(rows, rows + NG)

    @pl.when(pl.program_id(0) == 0)
    def _():
        bmid[...] = same_doc(idc_ref[mid, :], idr_ref[:, mid])
        gbias[...] = jnp.broadcast_to(kb_ref[...], gbias.shape)
        edge_biases(idc_ref, idr_ref, idh_ref, own, halo)

    product = (do_ref[...].astype(f32) * o_ref[...].astype(f32)).T
    delta = [product[HEAD_DIM * h : HEAD_DIM * (h + 1), :].sum(0, keepdims=True) for h in (0, 1)]
    lse = [lse_ref[0, h : h + 1, :] for h in (0, 1)]
    kg, vg = kg_ref[...], vg_ref[...]
    kgt, kt = kg.T, k_ref[...].T
    dq, dk, dv = attend_back(
        q_ref[mid, :] * bf16(SCALE), do_ref[mid, :], [x[:, mid] for x in lse], [x[:, mid] for x in delta],
        [k_ref[mid, :], kg], [kt[:, mid], kgt], [v_ref[mid, :], vg], [bmid, None],
    )
    dq_ref[mid, :] = dq.T.astype(bf16)
    dk_sum[mid, :], dv_sum[mid, :] = dk[0], dv[0]
    dkg, dvg = dk[1], dv[1]
    for side, half in edge_slices(rows):
        kh = kh_ref[half, :]
        dq, dk, dv = attend_back(
            q_ref[side, :] * bf16(SCALE), do_ref[side, :], [x[:, side] for x in lse], [x[:, side] for x in delta],
            [k_ref[side, :], kh, kg], [kt[:, side], kh.T, kgt],
            [v_ref[side, :], vh_ref[half, :], vg], [own.at[half], halo.at[half], None],
        )
        dq_ref[side, :] = dq.T.astype(bf16)
        dk_sum[side, :], dv_sum[side, :] = dk[0], dv[0]
        dkh_ref[half, :] = dk[1].astype(bf16)
        dvh_ref[half, :] = dv[1].astype(bf16)
        dkg, dvg = dkg + dk[2], dvg + dv[2]
    stat = [stat_ref[0, j : j + 1, :] for j in range(4)]
    dq, dk, dv = attend_back(
        qg_ref[...] * bf16(SCALE), dog_ref[...], stat[:2], stat[2:],
        [k_ref[...], kg], [kt, kgt], [v_ref[...], vg], [gbias.at[:rows], gbias.at[rows:]],
    )
    dq_ref[glob, :] = dq.T.astype(bf16)
    dk_ref[:rows, :] = (dk_sum[...] + dk[0]).astype(bf16)
    dv_ref[:rows, :] = (dv_sum[...] + dv[0]).astype(bf16)
    dk_ref[glob, :] = (dkg + dk[1]).astype(bf16)
    dv_ref[glob, :] = (dvg + dv[1]).astype(bf16)


def pair_cols(rows, block=0):
    return pl.BlockSpec((rows, LANES), lambda h: (block, h))


def whole(*shape):
    return pl.BlockSpec(shape, lambda h: (0,) * len(shape))


def pair_rows(count):
    return pl.BlockSpec((1, 8, count), lambda h: (h, 0, 0))


def struct(shape, kind):
    return jax.ShapeDtypeStruct(shape, kind)


def grant():
    return pltpu.CompilerParams(vmem_limit_bytes=60 << 20)


def cost(flops, size, exps=0):
    return pl.CostEstimate(flops=int(flops), bytes_accessed=int(size), transcendentals=int(exps))


def forward_mid(q, k, v, idc, idr, key_bias):
    rows, width = q.shape[0] - NG, q.shape[1]
    own, glob = pair_cols(rows), pair_cols(NG, rows // NG)
    return pl.pallas_call(
        forward_mid_kernel,
        grid=(PAIRS,),
        in_specs=[own, own, own, glob, glob, glob, whole(rows, 1), whole(1, rows), whole(rows + NG, 1)],
        out_specs=[pair_cols(rows - BLOCK), pair_rows(rows - BLOCK), pair_cols(NG), pair_rows(NG)],
        out_shape=[
            struct((rows - BLOCK, width), bf16), struct((PAIRS, 8, rows - BLOCK), f32),
            struct((NG, width), f32), struct((PAIRS, 8, NG), f32),
        ],
        scratch_shapes=[pltpu.VMEM((rows - BLOCK, rows - BLOCK), f32), pltpu.VMEM((rows + NG, NG), f32)],
        compiler_params=grant(),
        cost_estimate=cost(1.5e10, 8e6, 6e6),
        name="forward_mid",
    )(q, k, v, q, k, v, idc, idr, key_bias)


def forward_edge(q, k, v, kh, vh, idc, idr, idh):
    rows, width = q.shape[0] - NG, q.shape[1]
    own, glob, halo = pair_cols(rows), pair_cols(NG, rows // NG), pair_cols(BLOCK)
    return pl.pallas_call(
        forward_edge_kernel,
        grid=(PAIRS,),
        in_specs=[own, own, own, halo, halo, glob, glob, whole(rows, 1), whole(1, rows), whole(BLOCK, 1)],
        out_specs=[halo, pair_rows(BLOCK)],
        out_shape=[struct((BLOCK, width), bf16), struct((PAIRS, 8, BLOCK), f32)],
        scratch_shapes=[pltpu.VMEM((BLOCK, HALF), f32)] * 2,
        compiler_params=grant(),
        cost_estimate=cost(1.5e10, 8e6, 4e6),
        name="forward_edge",
    )(q, k, v, kh, vh, k, v, idc, idr, idh)


def backward(q, k, v, kh, vh, grad, out, grad_glob, lse, stat, idc, idr, idh, key_bias):
    rows, width = q.shape[0] - NG, q.shape[1]
    own, glob, halo, joint = pair_cols(rows), pair_cols(NG, rows // NG), pair_cols(BLOCK), pair_cols(rows + NG)
    return pl.pallas_call(
        backward_kernel,
        grid=(PAIRS,),
        in_specs=[
            own, own, own, glob, glob, glob, halo, halo, own, own, pair_cols(NG),
            pair_rows(rows), pair_rows(NG), whole(rows, 1), whole(1, rows), whole(BLOCK, 1), whole(rows + NG, 1),
        ],
        out_specs=[joint, joint, joint, halo, halo],
        out_shape=[struct((rows + NG, width), bf16)] * 3 + [struct((BLOCK, width), bf16)] * 2,
        scratch_shapes=[
            pltpu.VMEM((rows - BLOCK, rows - BLOCK), f32), pltpu.VMEM((BLOCK, HALF), f32),
            pltpu.VMEM((BLOCK, HALF), f32), pltpu.VMEM((rows + NG, NG), f32),
            pltpu.VMEM((rows, LANES), f32), pltpu.VMEM((rows, LANES), f32),
        ],
        compiler_params=grant(),
        cost_estimate=cost(4e10, 2e7, 1e7),
        name="backward_attention",
    )(q, k, v, q, k, v, kh, vh, grad, out, grad_glob, lse, stat, idc, idr, idh, key_bias)


def feed_kernel(n2_ref, dy_ref, wh_ref, wr_ref, res_ref, dn2_ref, dwh_ref, dwr_ref, n2t, dyt):
    @pl.when(pl.program_id(0) == 0)
    def _():
        n2t[...] = n2_ref[...].T
        dyt[...] = dy_ref[...].T
        res_ref[...] = jnp.zeros_like(res_ref)
        dn2_ref[...] = jnp.zeros_like(dn2_ref)

    wh, wr = wh_ref[...], wr_ref[...]
    pre = nn(n2_ref[...], wh)
    grad_act = nt(dy_ref[...], wr)
    below = 0.5 * (1.0 + lax.erf(pre * INV_SQRT2))
    density = jnp.exp(-0.5 * pre * pre) * INV_SQRT2PI
    act = (pre * below).astype(bf16)
    grad_pre = (grad_act * (below + pre * density)).astype(bf16)
    res_ref[...] += nn(act, wr)
    dn2_ref[...] += nt(grad_pre, wh)
    dwh_ref[...] = nn(n2t[...], grad_pre).astype(bf16)
    dwr_ref[...] = nn(dyt[...], act).astype(bf16).T


def feed_forward(n2, dy, wh, wr, chunk=512):
    rows, width = n2.shape
    hidden = wh.shape[1]
    wide, tall = pl.BlockSpec((width, chunk), lambda i: (0, i)), pl.BlockSpec((chunk, width), lambda i: (i, 0))
    return pl.pallas_call(
        feed_kernel,
        grid=(hidden // chunk,),
        in_specs=[whole(rows, width), whole(rows, width), wide, tall],
        out_specs=[whole(rows, width), whole(rows, width), wide, tall],
        out_shape=[
            struct((rows, width), f32), struct((rows, width), f32),
            struct((width, hidden), bf16), struct((hidden, width), bf16),
        ],
        scratch_shapes=[pltpu.VMEM((width, rows), bf16)] * 2,
        compiler_params=grant(),
        cost_estimate=cost(12 * rows * width * hidden, 3e7, 2 * rows * hidden),
        name="feed_forward",
    )(n2, dy, wh, wr)


def normalize(value):
    center = value - jnp.mean(value, axis=-1, keepdims=True)
    inverse = lax.rsqrt(jnp.mean(center * center, axis=-1, keepdims=True) + EPSILON)
    return center * inverse, inverse


def norm_back(unit, inverse, gain, grad):
    scaled = grad * gain
    mean_grad = jnp.mean(scaled, axis=-1, keepdims=True)
    mean_along = jnp.mean(scaled * unit, axis=-1, keepdims=True)
    return inverse * (scaled - mean_grad - unit * mean_along)


def document_ids(positions, starts, lengths):
    inside = (positions[:, None] >= starts[None, :]) & (positions[:, None] < (starts + lengths)[None, :])
    numbers = jnp.arange(1, starts.shape[0] + 1, dtype=jnp.int32)
    return jnp.sum(jnp.where(inside, numbers[None, :], 0), axis=1)


def pick(value, axis, index):
    return lax.dynamic_index_in_dim(value, index, axis, keepdims=False)


def scatter_sum(grad, swap):
    count = lax.axis_size("seq")
    bits = count.bit_length() - 1
    seq, core = lax.axis_index("seq"), lax.axis_index("batch")
    rows, cols = grad.shape
    kept = grad.reshape((count, 2, rows // (2 * count), cols))
    sent = lax.ppermute(pick(kept, 1, 1 - core), "batch", [(0, 1), (1, 0)])
    kept = pick(kept, 1, core).astype(f32) + sent.astype(f32)
    kept = kept.reshape((2,) * bits + kept.shape[1:])
    order = list(range(bits))
    if swap and bits > 1:
        order[0], order[1] = 1, 0
    left = list(range(bits - 1, -1, -1))
    for bit in order:
        axis = left.index(bit)
        mine = (seq >> bit) & 1
        step = [(i, i ^ (1 << bit)) for i in range(count)]
        sent = lax.ppermute(pick(kept, axis, 1 - mine).astype(bf16), "seq", step)
        kept = pick(kept, axis, mine) + sent.astype(f32)
        left.remove(bit)
    return kept


def exchange(value):
    return lax.all_to_all(value, "seq", 0, 0, tiled=True)


def gather_rows(value):
    return exchange(jnp.tile(value, (lax.axis_size("seq"), 1)))


def three_parts(value):
    parts = []
    for _ in range(3):
        part = lax.reduce_precision(value, 8, 7)
        parts.append(part.astype(bf16))
        value = value - part
    return parts


def per_head(value):
    return jnp.repeat(value, HEAD_DIM, axis=-1)


def shards(
    tokens, global_states, doc_starts, doc_lengths, first_gain, first_bias, query_weight, key_weight,
    value_weight, output_weight, second_gain, second_bias, hidden_weight, return_weight,
    output_cotangent, global_cotangent,
):
    rows, width = tokens.shape[1:]
    count = lax.axis_size("seq")
    share = NG // count
    pad = 16 - share
    seq = lax.axis_index("seq")
    forward = [(i, i + 1) for i in range(count - 1)]
    backward_route = [(b, a) for a, b in forward]
    own_rows = lambda value: lax.dynamic_slice_in_dim(value, seq * share, share, axis=0)
    join = lambda low, high: jnp.concatenate([low, high, jnp.zeros((pad, width), low.dtype)])

    halo_tokens = jnp.concatenate(
        [
            lax.ppermute(tokens[0, rows - HALF :], "seq", forward),
            lax.ppermute(tokens[0, :HALF], "seq", backward_route),
        ]
    )
    ident_all = document_ids(
        seq * rows - HALF + jnp.arange(rows + BLOCK, dtype=jnp.int32), doc_starts[0], doc_lengths[0]
    )
    ident = ident_all[HALF : HALF + rows]
    idc, idr = ident[:, None], ident[None, :]
    idh = jnp.concatenate([ident_all[:HALF], ident_all[HALF + rows :]])[:, None]
    key_bias = jnp.concatenate(
        [jnp.where(ident > 0, 0.0, MASKED), jnp.broadcast_to(jnp.where(seq == 0, 0.0, MASKED), (NG,))]
    ).astype(f32)[:, None]

    inputs = jnp.concatenate([tokens[0], global_states[0]]).astype(f32)
    unit, inverse = normalize(inputs)
    normed = (unit * first_gain + first_bias).astype(bf16)
    q = nn(normed, query_weight).astype(bf16)
    k = nn(normed, key_weight).astype(bf16)
    v = nn(normed, value_weight).astype(bf16)
    out_mid, lse_mid, out_glob, stat_glob = forward_mid(q, k, v, idc, idr, key_bias)

    peaks = stat_glob[:, :2].reshape(HEADS, NG).T
    totals = stat_glob[:, 2:4].reshape(HEADS, NG).T
    packed = jnp.concatenate(
        [out_glob, peaks, totals, jnp.zeros((NG, LANES - 2 * HEADS), f32)], axis=1
    )
    parts = exchange(packed).reshape(count, share, width + LANES)
    peaks, totals = parts[:, :, width : width + HEADS], parts[:, :, width + HEADS : width + 2 * HEADS]
    peak = jnp.max(peaks, axis=0)
    factor = jnp.exp(peaks - peak)
    total = jnp.sum(factor * totals, axis=0)
    lse_own = peak + jnp.log(total)
    out_own = jnp.sum(per_head(factor) * parts[:, :, :width], axis=0) / per_head(total)

    halo_unit, _ = normalize(halo_tokens.astype(f32))
    halo_normed = (halo_unit * first_gain + first_bias).astype(bf16)
    kh = nn(halo_normed, key_weight).astype(bf16)
    vh = nn(halo_normed, value_weight).astype(bf16)
    out_edge, lse_edge = forward_edge(q, k, v, kh, vh, idc, idr, idh)
    lse = jnp.concatenate([lse_edge[:, :, :HALF], lse_mid, lse_edge[:, :, HALF:]], axis=2)

    attended = jnp.concatenate(
        [out_edge[:HALF], out_mid, out_edge[HALF:], out_own.astype(bf16), jnp.zeros((pad, width), bf16)]
    )
    resid = join(inputs[:rows], own_rows(inputs[rows:])) + nn(attended, output_weight)
    unit_two, inverse_two = normalize(resid)
    normed_two = (unit_two * second_gain + second_bias).astype(bf16)
    grad_low = join(output_cotangent[0], own_rows(global_cotangent[0]))
    fed, grad_normed_two, hidden_part, return_part = feed_forward(
        normed_two, grad_low, hidden_weight, return_weight
    )
    result = (resid + fed).astype(bf16)
    second_gain_part = jnp.sum(grad_normed_two * unit_two, axis=0)
    second_bias_part = jnp.sum(grad_normed_two, axis=0)
    grad_resid = grad_low.astype(f32) + norm_back(unit_two, inverse_two, second_gain, grad_normed_two)
    grad_branch = grad_resid.astype(bf16)
    output_part = tn(attended, grad_branch).astype(bf16)
    grad_attended = nt(grad_branch, output_weight).astype(bf16)

    hidden_grad = scatter_sum(hidden_part, False)
    return_grad = scatter_sum(return_part, True)

    glob = slice(rows, rows + share)
    delta_own = jnp.sum(
        (grad_attended[glob].astype(f32) * out_own).reshape(share, HEADS, HEAD_DIM), axis=-1
    )
    figures = jnp.concatenate([lse_own, delta_own], axis=1)
    spread = jnp.concatenate(
        [grad_attended[glob], result[glob], *three_parts(figures),
         jnp.zeros((share, LANES - 6 * HEADS), bf16)], axis=1,
    )
    spread = gather_rows(spread)
    grad_glob, global_out = spread[:, :width], spread[:, width : 2 * width]
    figures = spread[:, 2 * width :].astype(f32)
    figures = figures[:, : 2 * HEADS] + figures[:, 2 * HEADS : 4 * HEADS] + figures[:, 4 * HEADS : 6 * HEADS]
    stat = figures.T.reshape(2, PAIRS, 2, NG).transpose(1, 0, 2, 3).reshape(PAIRS, 4, NG)
    stat = jnp.concatenate([stat, jnp.zeros_like(stat)], axis=1)

    dq, dk, dv, dkh, dvh = backward(
        q, k, v, kh, vh, grad_attended, attended, grad_glob, lse, stat, idc, idr, idh, key_bias
    )
    halo_part = nt(dkh, key_weight) + nt(dvh, value_weight)
    halo_low = halo_part.astype(bf16)
    from_next = lax.ppermute(halo_low[:HALF], "seq", backward_route)
    from_prev = lax.ppermute(halo_low[HALF:], "seq", forward)
    query_part = tn(normed, dq)
    key_part = tn(normed, dk) + tn(halo_normed, dkh)
    value_part = tn(normed, dv) + tn(halo_normed, dvh)
    grad_normed = nt(dq, query_weight) + nt(dk, key_weight) + nt(dv, value_weight)
    first_gain_part = jnp.sum(grad_normed * unit, axis=0) + jnp.sum(halo_part * halo_unit, axis=0)
    first_bias_part = jnp.sum(grad_normed, axis=0) + jnp.sum(halo_part, axis=0)
    vectors = jnp.stack([first_gain_part, first_bias_part, second_gain_part, second_bias_part], axis=1)
    vectors = jnp.concatenate([vectors, jnp.zeros((width, LANES - 4), f32)], axis=1)
    one = scatter_sum(jnp.concatenate([query_part, key_part], axis=1).astype(bf16), False)
    two = scatter_sum(
        jnp.concatenate([value_part.astype(bf16), output_part, vectors.astype(bf16)], axis=1), True
    )

    grad_tokens = grad_normed[:rows]
    grad_tokens = jnp.concatenate(
        [
            grad_tokens[:HALF] + from_prev.astype(f32),
            grad_tokens[HALF : rows - HALF],
            grad_tokens[rows - HALF :] + from_next.astype(f32),
        ]
    )
    tokens_grad = grad_resid[:rows] + norm_back(unit[:rows], inverse[:rows], first_gain, grad_tokens)
    grad_own = jnp.sum(exchange(grad_normed[rows:]).reshape(count, share, width), axis=0)
    grad_own = grad_resid[glob] + norm_back(
        own_rows(unit[rows:]), own_rows(inverse[rows:]), first_gain, grad_own
    )
    global_grad = gather_rows(grad_own)
    last = two[:, 2 * width :]
    return (
        result[:rows][None], global_out[None], tokens_grad[None], global_grad[None],
        last[:, 0], last[:, 1],
        one[:, :width], one[:, width:], two[:, :width], two[:, width : 2 * width],
        last[:, 2], last[:, 3],
        hidden_grad, return_grad,
    )


def solution(mesh):
    split, lone, spread = P("batch", "seq", None), P("batch", None, None), P(("seq", "batch"))
    return jax.shard_map(
        shards,
        mesh=mesh,
        in_specs=(split, lone, P("batch", None), P("batch", None)) + (P(),) * 10 + (split, lone),
        out_specs=(split, lone, split, lone) + (spread,) * 10,
        check_vma=False,
    )
```
